32 devices in a mesh: inv: 2 (over y), depth: 4 (over z), shot: 2 (over x), lat: 2 (over core).
Axes of the slice: x: 2, y: 2, z: 4, core: 2. Of those that a mesh axis runs over, the one named last changes fastest.
Arguments:
- model_field: float32 [128, 64, 128], P(('inv', 'depth'), 'lat'), parts along dimension 0, may hold values from 0.02 to 0.08
- buoyancy: float32 [128, 64, 128], P(('inv', 'depth'), 'lat'), parts along dimension 0, may hold values from 0.5 to 1.5
- forward_pair: float32 [4, 2, 64, 64, 128], P(('inv', 'shot'), None, 'depth', 'lat'), parts along dimension 0, may hold values from -6 to 6
- adjoint_pair: float32 [4, 2, 64, 64, 128], P(('inv', 'shot'), None, 'depth', 'lat'), parts along dimension 0, may hold values from -6 to 6
- stored_states: bfloat16 [4, 6, 64, 64, 128], P(('inv', 'shot'), None, 'depth', 'lat'), parts along dimension 0, may hold values from -6 to 6
- momentum: float32 [128, 64, 128], P(('inv', 'depth', 'shot'), 'lat'), parts along dimension 0, may hold values from -4 to 4
- wavelet: float32 [8, 4], P('inv'), parts along dimension 0, may hold values from -6 to 6
- residuals: float32 [8, 4, 256], P('inv'), parts along dimension 0, may hold values from -6 to 6
- source_cells: int32 [8], P('inv'), parts along dimension 0, may hold values from 0 to 524287
- receiver_cells: int32 [8, 256], P('inv'), parts along dimension 0, may hold values from 0 to 524287
- assignment: int32 [8], P('inv'), parts along dimension 0, may hold values from 0 to 3, each once
Outputs:
- forward_out: float32 [4, 2, 64, 64, 128], P(('inv', 'shot'), None, 'depth', 'lat'), parts along dimension 0
- adjoint_out: float32 [4, 2, 64, 64, 128], P(('inv', 'shot'), None, 'depth', 'lat'), parts along dimension 0
- momentum_new: float32 [128, 64, 128], P(('inv', 'depth', 'shot'), 'lat'), parts along dimension 0
- model_new: float32 [128, 64, 128], P(('inv', 'depth', 'shot'), 'lat'), parts along dimension 0
The draws below stay inside these ranges and needn't reach their ends.
There are 2 independent parts, one for each index of `inv`. The reference program is written for one: setup_inputs(seed, part) draws one part's arguments, and reference() takes and returns one part's arrays. A program takes and returns all parts, laid end to end along the dimension named above; each array names one. Nothing has to cross between parts.
Inputs may be any that keep to these rules, and one draw needn't show every extreme that they name: `source_cells`: flattened cell index of each shot's source. `receiver_cells`: flattened cell indices of each shot's receivers; cells may repeat. `assignment`: a permutation of the 4 shots.
All inputs are finite; a program needn't handle non-finite values.
Results may differ from the reference program's by a relative error of at most 0.0003.
Values sent between devices are 32-bit elements; how exact they have to be, the bound alone decides.
A program may use at most 64 MiB of HBM per device.

```python
import math
import jax
import jax.numpy as jnp

NX = 128
STEPS = 4
NREC = 256
NZ = 64
NY = 64
GROUPS = 2
SHOTS = 4


def with_ends(array, rng, smallest, high):
    longest = array.shape.index(max(array.shape))
    spots = []
    for shift in (0, 1):
        where = [jax.random.randint(jax.random.fold_in(rng, axis), (), 0, length) for axis, length in enumerate(array.shape)]
        where[longest] = (where[longest] + shift) % array.shape[longest]
        spots.append(tuple(where))
    return array.at[spots[0]].set(smallest).at[spots[1]].set(high)


def steps_of(stream_key, dims, cuts, smallest, top_value):
    def one(dim, parts):
        heights = jax.random.uniform(jax.random.fold_in(jax.random.fold_in(stream_key, 6), dim), (parts,), jnp.float32, smallest / len(cuts), top_value / len(cuts))
        return jnp.repeat(jnp.exp(heights), dims[dim] // parts).reshape((-1,) + (1,) * (len(dims) - dim - 1))

    loudness = one(*cuts[0])
    for cut in cuts[1:]:
        loudness = loudness * one(*cut)
    return loudness


def bell_draw(key, dims, width, limit, shards=(), held_as=jnp.bfloat16):
    values = jax.random.normal(key, dims, jnp.float32) * width
    if len(shards) > 0:
        values = steps_of(key, dims, shards, -0.22, 0.18) * values
    return jnp.clip(values, min=-limit, max=limit).astype(held_as)


def setup_inputs(seed: int = 0, part: int = 0) -> dict:
    key_list = jax.random.split(jax.random.key(seed), 12)
    own_keys = jax.random.split(jax.random.fold_in(key_list[11], part), 12)
    model_field = jnp.clip(0.02 + 0.06 * jax.random.uniform(own_keys[0], (NZ, NY, NX), jnp.float32) ** steps_of(own_keys[0], (NZ, NY, NX), ((0, 4), (1, 2)), -0.2, 0.2), 0.02, 0.08)
    buoyancy = jnp.clip(jnp.exp(math.log(1.5) - 1.0986123 * jax.random.uniform(own_keys[1], (NZ, NY, NX), jnp.float32) ** steps_of(own_keys[1], (NZ, NY, NX), ((0, 4), (1, 2)), -0.2, 0.2)), 0.5, 1.5)
    forward_pair = bell_draw(own_keys[2], (GROUPS, 2, NZ, NY, NX), 1.0, 6.0, ((0, 2), (2, 4), (3, 2)), jnp.float32)
    adjoint_pair = bell_draw(own_keys[3], (GROUPS, 2, NZ, NY, NX), 1.0, 6.0, ((0, 2), (2, 4), (3, 2)), jnp.float32)
    stored_states = bell_draw(own_keys[4], (GROUPS, STEPS + 2, NZ, NY, NX), 1.0, 6.0, ((0, 2), (2, 4), (3, 2)))
    momentum = bell_draw(own_keys[5], (NZ, NY, NX), 0.5, 4.0, ((0, 8), (1, 2)), jnp.float32)
    wavelet = bell_draw(own_keys[6], (SHOTS, STEPS), 1.0, 6.0, (), jnp.float32)
    residuals = bell_draw(own_keys[7], (SHOTS, STEPS, NREC), 1.0, 6.0, (), jnp.float32)
    source_cells = with_ends(jax.random.randint(own_keys[8], (SHOTS,), 0, NZ * NY * NX), jax.random.fold_in(own_keys[8], 1), 0, (NZ * NY * NX) - 1).astype(jnp.int32)
    receiver_cells = with_ends(jax.random.randint(own_keys[9], (SHOTS, NREC), 0, NZ * NY * NX), jax.random.fold_in(own_keys[9], 1), 0, (NZ * NY * NX) - 1).astype(jnp.int32)
    assignment = jax.random.permutation(own_keys[10], SHOTS).astype(jnp.int32)
    return dict(model_field=model_field, buoyancy=buoyancy, forward_pair=forward_pair, adjoint_pair=adjoint_pair, stored_states=stored_states, momentum=momentum, wavelet=wavelet, residuals=residuals, source_cells=source_cells, receiver_cells=receiver_cells, assignment=assignment)


SECOND_TAPS = (8.0 / 5.0, -1.0 / 5.0, 8.0 / 315.0, -1.0 / 560.0)
CENTER_TAP = -205.0 / 72.0
FIRST_TAPS = (4.0 / 5.0, -1.0 / 5.0, 4.0 / 105.0, -1.0 / 280.0)
MOMENT_KEEP = 0.9
STEP_RATE = 0.02


def offset_core(padded, along_axis, offset):
    pieces = [slice(None)] * (padded.ndim - 3)
    for axis_id in range(3):
        length = padded.shape[padded.ndim - 3 + axis_id] - 8
        begin = 4 + (offset if axis_id == along_axis else 0)
        pieces.append(slice(begin, begin + length))
    return padded[tuple(pieces)]


def second_sum(padded):
    total = 3.0 * CENTER_TAP * offset_core(padded, 0, 0)
    for axis_id in range(3):
        for reach in range(1, 5):
            total = total + SECOND_TAPS[reach - 1] * (offset_core(padded, axis_id, reach) + offset_core(padded, axis_id, -reach))
    return total


def first_diff(padded, axis_id):
    total = FIRST_TAPS[0] * (offset_core(padded, axis_id, 1) - offset_core(padded, axis_id, -1))
    for reach in range(2, 5):
        total = total + FIRST_TAPS[reach - 1] * (offset_core(padded, axis_id, reach) - offset_core(padded, axis_id, -reach))
    return total


def operator(padded, buoy_core, slopes):
    result = buoy_core * second_sum(padded)
    for axis_id in range(3):
        result = result + slopes[axis_id] * first_diff(padded, axis_id)
    return result


def inject(field, cell_ids, amounts):
    rows_all = field.shape[1]
    columns = field.shape[2]
    depth_index = cell_ids // (rows_all * columns)
    row_index = (cell_ids // columns) % rows_all
    column_index = cell_ids % columns
    return field.at[depth_index, row_index, column_index].add(amounts)


def reference(model_field, buoyancy, forward_pair, adjoint_pair, stored_states, momentum, wavelet, residuals, source_cells, receiver_cells, assignment):
    groups = forward_pair.shape[0]
    buoy_pad = jnp.pad(buoyancy, 4)
    slopes = tuple(first_diff(buoy_pad, axis_id) for axis_id in range(3))

    def advance(previous, current):
        padded = jnp.pad(current, 4)
        return 2.0 * current - previous + model_field * operator(padded, buoyancy, slopes)

    factor = 1.0 / (groups * STEPS)
    gradient = jnp.zeros(model_field.shape, jnp.float32)
    forward_list = []
    adjoint_list = []
    for group in range(groups):
        fwd_shot = assignment[group]
        adj_shot = assignment[groups + group]
        fwd_prev = forward_pair[group, 0]
        fwd_cur = forward_pair[group, 1]
        adj_prev = adjoint_pair[group, 0]
        adj_cur = adjoint_pair[group, 1]
        imaging = jnp.zeros(model_field.shape, jnp.float32)
        for step in range(STEPS):
            states = stored_states[group, step:step + 3].astype(jnp.float32)
            imaging = imaging + adj_cur * (states[2] - 2.0 * states[1] + states[0])
            fwd_next = inject(advance(fwd_prev, fwd_cur), source_cells[fwd_shot][None], wavelet[fwd_shot, step][None])
            adj_next = inject(advance(adj_prev, adj_cur), receiver_cells[adj_shot], residuals[adj_shot, step])
            fwd_prev, fwd_cur = fwd_cur, fwd_next
            adj_prev, adj_cur = adj_cur, adj_next
        gradient = gradient + imaging * factor
        forward_list.append(jnp.stack([fwd_prev, fwd_cur]))
        adjoint_list.append(jnp.stack([adj_prev, adj_cur]))
    momentum_new = MOMENT_KEEP * momentum + gradient
    model_new = model_field - STEP_RATE * momentum_new
    return jnp.stack(forward_list), jnp.stack(adjoint_list), momentum_new, model_new
```

```python
import functools
import jax
import jax.numpy as jnp
from jax import lax
from jax.experimental import pallas as pl
from jax.experimental.pallas import tpu as pltpu
from jax.sharding import PartitionSpec as P

SECOND_TAPS = (8.0 / 5.0, -1.0 / 5.0, 8.0 / 315.0, -1.0 / 560.0)
CENTER_TAP = -205.0 / 72.0
FIRST_TAPS = (4.0 / 5.0, -1.0 / 5.0, 4.0 / 105.0, -1.0 / 280.0)
MOMENT_KEEP = 0.9
STEP_RATE = 0.02
MESH = pl.DeviceIdType.MESH
BF = jnp.bfloat16
F32 = jnp.float32
FWD, ADJ = 0, 1


def split_div(value, size):
    if size & (size - 1) == 0:
        bits = size.bit_length() - 1
        return lax.shift_right_logical(value, bits), value & (size - 1)
    whole = lax.div(value, size)
    return whole, value - whole * size


def kernel(
    dims,
    assign_ref, source_ref, wave_ref, recv_ref, resid_ref,
    model_ref, buoy_ref, fpair_ref, apair_ref, states_ref, mom_ref,
    fout_ref, aout_ref, momout_ref, modout_ref,
    ext, bext, model_v, states_v, mom_v, coef, inj, xder, img, share, momnew, modnew, wmat,
    zsend, zrecv, ysend, yrecv, bsend, brecv, ssend, srecv, load, store,
):
    groups, n_depth, n_lat, planes, rows, cols, steps, n_rec = dims
    rows_all = rows * n_lat
    q = planes // groups
    d = lax.axis_index("depth")
    l = lax.axis_index("lat")
    s = lax.axis_index("shot")
    pairs = (fpair_ref, apair_ref)
    core_p = pl.ds(4, planes)
    core_r = pl.ds(8, rows)
    has = {
        ("depth", 0): d > 0,
        ("depth", 1): d < n_depth - 1,
        ("lat", 0): l > 0,
        ("lat", 1): l < n_lat - 1,
    }
    rank = {"depth": d, "lat": l}

    loads = {}

    def begin(name, src, dst):
        loads[name] = pltpu.make_async_copy(src, dst, load.at[len(loads)])
        loads[name].start()

    begin("buoy", buoy_ref, bext.at[core_p, core_r])
    begin("model", model_ref, model_v)
    for f in (ADJ, FWD):
        begin(("cur", f), pairs[f].at[0, 1], ext.at[0, f, core_p, core_r])
        begin(("prev", f), pairs[f].at[0, 0], ext.at[1, f, core_p, core_r])
    begin("states", states_ref.at[0], states_v)
    begin("mom", mom_ref, mom_v)

    for lo in (0, planes + 4):
        for slot in range(2):
            for f in range(2):
                ext[slot, f, pl.ds(lo, 4), core_r] = jnp.zeros((4, rows, cols), F32)
        bext[pl.ds(lo, 4), core_r] = jnp.zeros((4, rows, cols), F32)
    for lo in (0, rows + 8):
        for slot in range(2):
            for f in range(2):
                ext[slot, f, core_p, pl.ds(lo, 8)] = jnp.zeros((planes, 8, cols), F32)
        bext[core_p, pl.ds(lo, 8)] = jnp.zeros((planes, 8, cols), F32)

    barrier = pltpu.get_barrier_semaphore()
    total = groups - 1
    for (axis, way), there in has.items():
        total = total + there.astype(jnp.int32)

        @pl.when(there)
        def _(axis=axis, way=way):
            pl.semaphore_signal(
                barrier, inc=1, device_id={axis: rank[axis] + 2 * way - 1}, device_id_type=MESH
            )

    for o in range(1, groups):
        pl.semaphore_signal(
            barrier, inc=1, device_id={"shot": lax.rem(s + o, groups)}, device_id_type=MESH
        )
    pl.semaphore_wait(barrier, total)

    def remote(src, dst, send, recv, axis, way):
        return pltpu.make_async_remote_copy(
            src_ref=src, dst_ref=dst, send_sem=send, recv_sem=recv,
            device_id={axis: rank[axis] + 2 * way - 1}, device_id_type=MESH,
        )

    chunks = ((0, 4), (planes - 4, 4)) + (((4, planes - 8),) if planes > 8 else ())

    def zcopy(e, f, way):
        slot = e % 2
        first = planes - 4 if way else 0
        if e == 0:
            src = pairs[f].at[0, 1, pl.ds(first, 4)]
        else:
            src = ext.at[slot, f, pl.ds(4 + first, 4), core_r]
        dst = ext.at[slot, f, pl.ds(0 if way else planes + 4, 4), core_r]
        return remote(src, dst, zsend.at[e, f, way], zrecv.at[e, f, way], "depth", way)

    def ycopy(e, f, c, way):
        slot = e % 2
        first, count = chunks[c]
        row = rows - 8 if way else 0
        if e == 0:
            src = pairs[f].at[0, 1, pl.ds(first, count), pl.ds(row, 8)]
        else:
            src = ext.at[slot, f, pl.ds(4 + first, count), pl.ds(8 + row, 8)]
        dst = ext.at[slot, f, pl.ds(4 + first, count), pl.ds(0 if way else rows + 8, 8)]
        return remote(src, dst, ysend.at[e, f, c, way], yrecv.at[e, f, c, way], "lat", way)

    def bcopy(axis, way):
        a = 0 if axis == "depth" else 1
        if a == 0:
            src = buoy_ref.at[pl.ds(planes - 4 if way else 0, 4)]
            dst = bext.at[pl.ds(0 if way else planes + 4, 4), core_r]
        else:
            src = buoy_ref.at[:, pl.ds(rows - 8 if way else 0, 8)]
            dst = bext.at[core_p, pl.ds(0 if way else rows + 8, 8)]
        return remote(src, dst, bsend.at[a, way], brecv.at[a, way], axis, way)

    def start(copy, axis, way):
        @pl.when(has[(axis, way)])
        def _():
            copy.start()

    def wait_send(copy, axis, way):
        @pl.when(has[(axis, way)])
        def _():
            copy.wait_send()

    def wait_recv(copy, axis, way):
        @pl.when(has[(axis, 1 - way)])
        def _():
            copy.wait_recv()

    for way in (0, 1):
        start(bcopy("depth", way), "depth", way)
        start(bcopy("lat", way), "lat", way)
    for f in (ADJ, FWD):
        for way in (0, 1):
            start(zcopy(0, f, way), "depth", way)
            for c in range(len(chunks)):
                start(ycopy(0, f, c, way), "lat", way)

    delta = lax.broadcasted_iota(jnp.int32, (cols, cols), 0) - lax.broadcasted_iota(
        jnp.int32, (cols, cols), 1
    )
    second = jnp.where(delta == 0, 3.0 * CENTER_TAP, 0.0).astype(F32)
    first = jnp.zeros((cols, cols), F32)
    for reach in range(1, 5):
        second = jnp.where(jnp.abs(delta) == reach, SECOND_TAPS[reach - 1], second)
        first = jnp.where(delta == reach, FIRST_TAPS[reach - 1], first)
        first = jnp.where(delta == -reach, -FIRST_TAPS[reach - 1], first)
    for a, mat in ((0, second), (1, first)):
        high = mat.astype(BF)
        low = (mat - high.astype(F32)).astype(BF)
        wmat[pl.ds(0, cols), pl.ds(a * cols, cols)] = high
        wmat[pl.ds(cols, cols), pl.ds(a * cols, cols)] = high
        wmat[pl.ds(2 * cols, cols), pl.ds(a * cols, cols)] = low

    fshot = assign_ref[s]
    ashot = assign_ref[groups + s]
    cells = recv_ref[pl.ds(ashot, 1), :]
    line, column = split_div(cells, cols)
    depth_id, row_id = split_div(line, rows_all)
    depth_id = depth_id - d * planes
    row_id = row_id - l * rows
    inside = (depth_id >= 0) & (depth_id < planes) & (row_id >= 0) & (row_id < rows)
    where_row = jnp.where(inside, depth_id * rows + row_id, -1)
    row_hot = jnp.where(
        lax.broadcasted_iota(jnp.int32, (planes * rows, n_rec), 0) == where_row, 1.0, 0.0
    ).astype(BF)
    col_hit = lax.broadcasted_iota(jnp.int32, (cols, n_rec), 0) == column
    traces = resid_ref[ashot]
    contract = (((1,), (1,)), ((), ()))
    for k in range(steps):
        part = jnp.where(col_hit, traces[k : k + 1, :], 0.0)
        amount = None
        for _ in range(3):
            piece = part.astype(BF)
            part = part - piece.astype(F32)
            term = lax.dot_general(row_hot, piece, contract, preferred_element_type=F32)
            amount = term if amount is None else amount + term
        inj[k] = amount.reshape(planes, rows, cols)

    sline, scol = split_div(source_ref[fshot], cols)
    sdepth, srow = split_div(sline, rows_all)
    sdepth = sdepth - d * planes
    srow = srow - l * rows
    sinside = (srow >= 0) & (srow < rows)
    sdepth = jnp.where(sinside, sdepth, -1)
    cell_ids = lax.broadcasted_iota(jnp.int32, (rows, cols), 0) * cols + lax.broadcasted_iota(
        jnp.int32, (rows, cols), 1
    )
    scell = srow * cols + scol

    def x_part(block):
        count = block.shape[0]
        block = block.reshape(count * rows, cols)
        high = block.astype(BF)
        low = (block - high.astype(F32)).astype(BF)
        lhs = jnp.concatenate([high, low, high], axis=1)
        return jnp.dot(lhs, wmat[...], preferred_element_type=F32)

    def imaging(k):
        def body(p, carry):
            older = states_v[k, p].astype(F32)
            mid = states_v[k + 1, p].astype(F32)
            newer = states_v[k + 2, p].astype(F32)
            term = ext[k % 2, ADJ, p + 4, core_r] * (newer - 2.0 * mid + older)
            img[p] = term if k == 0 else img[p] + term
            return carry

        lax.fori_loop(0, planes, body, 0)

    def diffs(pick, want_second):
        first = None
        second = None
        for reach in range(1, 5):
            ahead, behind = pick(reach), pick(-reach)
            term = FIRST_TAPS[reach - 1] * (ahead - behind)
            first = term if first is None else first + term
            if want_second:
                term = SECOND_TAPS[reach - 1] * (ahead + behind)
                second = term if second is None else second + term
        return first, second

    def coefficients(p0):
        xs = x_part(bext[pl.ds(p0 + 4, 4), core_r])
        for i in range(4):
            p = p0 + i
            m = model_v[p]
            sz, _ = diffs(lambda o: bext[p + 4 + o, core_r], False)
            sy, _ = diffs(lambda o: bext[p + 4, pl.ds(8 + o, rows)], False)
            coef[0, p] = m * bext[p + 4, core_r]
            coef[1, p] = m * sz
            coef[2, p] = m * sy
            coef[3, p] = m * xs[i * rows : (i + 1) * rows, cols:]

    def advance(k, f, p0):
        now, then = k % 2, (k + 1) % 2
        xder[...] = x_part(ext[now, f, pl.ds(p0 + 4, 4), core_r])
        for i in range(4):
            p = p0 + i
            fz, gz = diffs(lambda o: ext[now, f, p + 4 + o, core_r], True)
            fy, gy = diffs(lambda o: ext[now, f, p + 4, pl.ds(8 + o, rows)], True)
            xrow = pl.ds(i * rows, rows)
            second = gz + gy + xder[xrow, pl.ds(0, cols)]
            value = (
                2.0 * ext[now, f, p + 4, core_r]
                - ext[then, f, p + 4, core_r]
                + coef[0, p] * second
                + coef[1, p] * fz
                + coef[2, p] * fy
                + coef[3, p] * xder[xrow, pl.ds(cols, cols)]
            )
            if f == ADJ:
                value = value + inj[k, p]
            else:
                here = jnp.where(sdepth == p, scell, -1)
                value = value + jnp.where(cell_ids == here, wave_ref[fshot, k], 0.0)
            ext[then, f, p + 4, core_r] = value

    loads["states"].wait()
    loads[("cur", ADJ)].wait()
    imaging(0)
    loads["model"].wait()
    loads["buoy"].wait()
    for way in (0, 1):
        wait_recv(bcopy("lat", way), "lat", way)
        wait_recv(bcopy("depth", way), "depth", way)

    def coef_body(c, carry):
        coefficients(c * 4)
        return carry

    lax.fori_loop(0, planes // 4, coef_body, 0)
    loads[("prev", ADJ)].wait()
    loads[("cur", FWD)].wait()
    loads[("prev", FWD)].wait()

    outs = (fout_ref, aout_ref)
    finals = []

    def share_copy(o):
        dest = lax.rem(s + o, groups)
        return pltpu.make_async_remote_copy(
            src_ref=img.at[pl.ds(dest * q, q)], dst_ref=share.at[o - 1],
            send_sem=ssend.at[o - 1], recv_sem=srecv.at[o - 1],
            device_id={"shot": dest}, device_id_type=MESH,
        )

    def finish(src, dst):
        copy = pltpu.make_async_copy(src, dst, store.at[len(finals)])
        copy.start()
        finals.append(copy)

    for k in range(steps):
        last = k == steps - 1
        if k > 0:
            imaging(k)
        if last:
            for o in range(1, groups):
                share_copy(o).start()
            for f in (ADJ, FWD):
                finish(ext.at[k % 2, f, core_p, core_r], outs[f].at[0, 0])
        for f in (ADJ, FWD):
            if k >= 2:
                for way in (0, 1):
                    wait_send(zcopy(k - 1, f, way), "depth", way)
                    for c in range(len(chunks)):
                        wait_send(ycopy(k - 1, f, c, way), "lat", way)
            for c in (0, 1):
                for way in (0, 1):
                    wait_recv(ycopy(k, f, c, way), "lat", way)
                wait_recv(zcopy(k, f, 1 - c), "depth", 1 - c)
                advance(k, f, chunks[c][0])
                if not last:
                    start(zcopy(k + 1, f, c), "depth", c)
                    for way in (0, 1):
                        start(ycopy(k + 1, f, c, way), "lat", way)
        for f in (ADJ, FWD):
            if len(chunks) > 2:
                for way in (0, 1):
                    wait_recv(ycopy(k, f, 2, way), "lat", way)

                def inner(c, carry):
                    advance(k, f, 4 + c * 4)
                    return carry

                lax.fori_loop(0, (planes - 8) // 4, inner, 0)
                if not last:
                    for way in (0, 1):
                        start(ycopy(k + 1, f, 2, way), "lat", way)
            if last:
                finish(ext.at[(k + 1) % 2, f, core_p, core_r], outs[f].at[0, 1])

    loads["mom"].wait()
    for o in range(1, groups):
        share_copy(o).wait_recv()
    factor = 1.0 / (groups * steps)
    for p in range(q):
        gradient = img[s * q + p]
        for o in range(1, groups):
            gradient = gradient + share[o - 1, p]
        moment = MOMENT_KEEP * mom_v[p] + factor * gradient
        momnew[p] = moment
        modnew[p] = model_v[s * q + p] - STEP_RATE * moment
    finish(momnew, momout_ref)
    finish(modnew, modout_ref)
    for o in range(1, groups):
        share_copy(o).wait_send()
    for way in (0, 1):
        wait_send(bcopy("depth", way), "depth", way)
        wait_send(bcopy("lat", way), "lat", way)
    for e in sorted({0, steps - 1}):
        for f in (ADJ, FWD):
            for way in (0, 1):
                wait_send(zcopy(e, f, way), "depth", way)
                for c in range(len(chunks)):
                    wait_send(ycopy(e, f, c, way), "lat", way)
    for copy in finals:
        copy.wait()


def local(
    model_field, buoyancy, forward_pair, adjoint_pair, stored_states, momentum,
    wavelet, residuals, source_cells, receiver_cells, assignment,
):
    groups = lax.axis_size("shot")
    n_depth = lax.axis_size("depth")
    n_lat = lax.axis_size("lat")
    planes, rows, cols = model_field.shape
    steps = stored_states.shape[1] - 2
    n_rec = receiver_cells.shape[1]
    q = planes // groups
    dims = (groups, n_depth, n_lat, planes, rows, cols, steps, n_rec)
    smem = pl.BlockSpec(memory_space=pltpu.SMEM)
    vmem = pl.BlockSpec(memory_space=pltpu.VMEM)
    hbm = pl.BlockSpec(memory_space=pl.ANY)
    dma = pltpu.SemaphoreType.DMA
    block = (planes, rows, cols)
    others = max(groups - 1, 1)
    out = pl.pallas_call(
        functools.partial(kernel, dims),
        out_shape=(
            jax.ShapeDtypeStruct(forward_pair.shape, F32),
            jax.ShapeDtypeStruct(adjoint_pair.shape, F32),
            jax.ShapeDtypeStruct(momentum.shape, F32),
            jax.ShapeDtypeStruct(momentum.shape, F32),
        ),
        in_specs=[smem, smem, smem, vmem, vmem] + [hbm] * 6,
        out_specs=(hbm,) * 4,
        scratch_shapes=[
            pltpu.VMEM((2, 2, planes + 8, rows + 16, cols), F32),
            pltpu.VMEM((planes + 8, rows + 16, cols), F32),
            pltpu.VMEM(block, F32),
            pltpu.VMEM((steps + 2,) + block, BF),
            pltpu.VMEM((q, rows, cols), F32),
            pltpu.VMEM((4,) + block, F32),
            pltpu.VMEM((steps,) + block, F32),
            pltpu.VMEM((4 * rows, 2 * cols), F32),
            pltpu.VMEM(block, F32),
            pltpu.VMEM((others, q, rows, cols), F32),
            pltpu.VMEM((q, rows, cols), F32),
            pltpu.VMEM((q, rows, cols), F32),
            pltpu.VMEM((3 * cols, 2 * cols), BF),
            dma((steps, 2, 2)), dma((steps, 2, 2)),
            dma((steps, 2, 3, 2)), dma((steps, 2, 3, 2)),
            dma((2, 2)), dma((2, 2)),
            dma((others,)), dma((others,)),
            dma((8,)), dma((6,)),
        ],
        compiler_params=pltpu.CompilerParams(collective_id=0, has_side_effects=True),
    )(
        assignment, source_cells, wavelet, receiver_cells, residuals,
        model_field, buoyancy, forward_pair, adjoint_pair, stored_states, momentum,
    )
    return tuple(out)


def solution(mesh):
    in_specs = (
        P(("inv", "depth"), "lat", None),
        P(("inv", "depth"), "lat", None),
        P(("inv", "shot"), None, "depth", "lat", None),
        P(("inv", "shot"), None, "depth", "lat", None),
        P(("inv", "shot"), None, "depth", "lat", None),
        P(("inv", "depth", "shot"), "lat", None),
        P("inv", None),
        P("inv", None, None),
        P("inv"),
        P("inv", None),
        P("inv"),
    )
    out_specs = (
        P(("inv", "shot"), None, "depth", "lat", None),
        P(("inv", "shot"), None, "depth", "lat", None),
        P(("inv", "depth", "shot"), "lat", None),
        P(("inv", "depth", "shot"), "lat", None),
    )
    return jax.shard_map(local, mesh=mesh, in_specs=in_specs, out_specs=out_specs, check_vma=False)
```

```python
import functools
import jax
import jax.numpy as jnp
from jax import lax
from jax.experimental import pallas as pl
from jax.experimental.pallas import tpu as pltpu
from jax.sharding import PartitionSpec as P

SECOND_TAPS = (8.0 / 5.0, -1.0 / 5.0, 8.0 / 315.0, -1.0 / 560.0)
CENTER_TAP = -205.0 / 72.0
FIRST_TAPS = (4.0 / 5.0, -1.0 / 5.0, 4.0 / 105.0, -1.0 / 280.0)
MOMENT_KEEP = 0.9
STEP_RATE = 0.02
MESH = pl.DeviceIdType.MESH
BF = jnp.bfloat16
F32 = jnp.float32
FWD, ADJ = 0, 1
VMEM_WINDOW = 61 * 1024 * 1024
VMEM_OUT = 24 * 1024 * 1024


def split_div(value, size):
    if size & (size - 1) == 0:
        bits = size.bit_length() - 1
        return lax.shift_right_logical(value, bits), value & (size - 1)
    whole = lax.div(value, size)
    return whole, value - whole * size


def kernel(
    dims,
    assign_ref, source_ref, wave_ref, recv_ref, resid_ref,
    model_ref, buoy_ref, fpair_ref, apair_ref, states_ref, mom_ref,
    fout_ref, aout_ref, momout_ref, modout_ref,
    ext, bext, model_v, states_v, mom_v, coef, inj, xder, img, share, wmat,
    zsend, zrecv, ysend, yrecv, bsend, brecv, ssend, srecv, load,
):
    groups, n_depth, n_lat, planes, rows, cols, steps, n_rec = dims
    rows_all = rows * n_lat
    q = planes // groups
    d = lax.axis_index("depth")
    l = lax.axis_index("lat")
    s = lax.axis_index("shot")
    pairs = (fpair_ref, apair_ref)
    outs = (fout_ref, aout_ref)
    core_p = pl.ds(4, planes)
    core_r = pl.ds(8, rows)
    has = {
        ("depth", 0): d > 0,
        ("depth", 1): d < n_depth - 1,
        ("lat", 0): l > 0,
        ("lat", 1): l < n_lat - 1,
    }
    rank = {"depth": d, "lat": l}

    loads = {}

    def begin(name, src, dst):
        loads[name] = pltpu.make_async_copy(src, dst, load.at[len(loads)])
        loads[name].start()

    begin("buoy", buoy_ref, bext.at[core_p, core_r])
    begin("model", model_ref, model_v)
    for f in (ADJ, FWD):
        begin(("cur", f), pairs[f].at[0, 1], ext.at[0, f, core_p, core_r])
        begin(("prev", f), pairs[f].at[0, 0], ext.at[1, f, core_p, core_r])
    begin("states", states_ref.at[0], states_v)
    begin("mom", mom_ref, mom_v)

    for lo in (0, planes + 4):
        for slot in range(2):
            for f in range(2):
                ext[slot, f, pl.ds(lo, 4), core_r] = jnp.zeros((4, rows, cols), F32)
        bext[pl.ds(lo, 4), core_r] = jnp.zeros((4, rows, cols), F32)
    for lo in (0, rows + 8):
        for slot in range(2):
            for f in range(2):
                ext[slot, f, core_p, pl.ds(lo, 8)] = jnp.zeros((planes, 8, cols), F32)
        bext[core_p, pl.ds(lo, 8)] = jnp.zeros((planes, 8, cols), F32)

    barrier = pltpu.get_barrier_semaphore()
    total = groups - 1
    for (axis, way), there in has.items():
        total = total + there.astype(jnp.int32)

        @pl.when(there)
        def _(axis=axis, way=way):
            pl.semaphore_signal(
                barrier, inc=1, device_id={axis: rank[axis] + 2 * way - 1}, device_id_type=MESH
            )

    for o in range(1, groups):
        pl.semaphore_signal(
            barrier, inc=1, device_id={"shot": lax.rem(s + o, groups)}, device_id_type=MESH
        )
    pl.semaphore_wait(barrier, total)

    def remote(src, dst, send, recv, axis, way):
        return pltpu.make_async_remote_copy(
            src_ref=src, dst_ref=dst, send_sem=send, recv_sem=recv,
            device_id={axis: rank[axis] + 2 * way - 1}, device_id_type=MESH,
        )

    chunks = ((0, 4), (planes - 4, 4)) + (((4, planes - 8),) if planes > 8 else ())

    def zcopy(e, f, way):
        slot = e % 2
        first = planes - 4 if way else 0
        if e == 0:
            src = pairs[f].at[0, 1, pl.ds(first, 4)]
        else:
            src = ext.at[slot, f, pl.ds(4 + first, 4), core_r]
        dst = ext.at[slot, f, pl.ds(0 if way else planes + 4, 4), core_r]
        return remote(src, dst, zsend.at[e, f, way], zrecv.at[e, f, way], "depth", way)

    def ycopy(e, f, c, way):
        slot = e % 2
        first, count = chunks[c]
        row = rows - 8 if way else 0
        if e == 0:
            src = pairs[f].at[0, 1, pl.ds(first, count), pl.ds(row, 8)]
        else:
            src = ext.at[slot, f, pl.ds(4 + first, count), pl.ds(8 + row, 8)]
        dst = ext.at[slot, f, pl.ds(4 + first, count), pl.ds(0 if way else rows + 8, 8)]
        return remote(src, dst, ysend.at[e, f, c, way], yrecv.at[e, f, c, way], "lat", way)

    def bcopy(axis, way):
        a = 0 if axis == "depth" else 1
        if a == 0:
            src = buoy_ref.at[pl.ds(planes - 4 if way else 0, 4)]
            dst = bext.at[pl.ds(0 if way else planes + 4, 4), core_r]
        else:
            src = buoy_ref.at[:, pl.ds(rows - 8 if way else 0, 8)]
            dst = bext.at[core_p, pl.ds(0 if way else rows + 8, 8)]
        return remote(src, dst, bsend.at[a, way], brecv.at[a, way], axis, way)

    def start(copy, axis, way):
        @pl.when(has[(axis, way)])
        def _():
            copy.start()

    def wait_send(copy, axis, way):
        @pl.when(has[(axis, way)])
        def _():
            copy.wait_send()

    def wait_recv(copy, axis, way):
        @pl.when(has[(axis, 1 - way)])
        def _():
            copy.wait_recv()

    for way in (0, 1):
        start(bcopy("depth", way), "depth", way)
        start(bcopy("lat", way), "lat", way)
    for f in (ADJ, FWD):
        for way in (0, 1):
            start(zcopy(0, f, way), "depth", way)
            for c in range(len(chunks)):
                start(ycopy(0, f, c, way), "lat", way)

    delta = lax.broadcasted_iota(jnp.int32, (cols, cols), 0) - lax.broadcasted_iota(
        jnp.int32, (cols, cols), 1
    )
    second = jnp.where(delta == 0, 3.0 * CENTER_TAP, 0.0).astype(F32)
    first = jnp.zeros((cols, cols), F32)
    for reach in range(1, 5):
        second = jnp.where(jnp.abs(delta) == reach, SECOND_TAPS[reach - 1], second)
        first = jnp.where(delta == reach, FIRST_TAPS[reach - 1], first)
        first = jnp.where(delta == -reach, -FIRST_TAPS[reach - 1], first)
    for a, mat in ((0, second), (1, first)):
        high = mat.astype(BF)
        low = (mat - high.astype(F32)).astype(BF)
        wmat[pl.ds(0, cols), pl.ds(a * cols, cols)] = high
        wmat[pl.ds(cols, cols), pl.ds(a * cols, cols)] = high
        wmat[pl.ds(2 * cols, cols), pl.ds(a * cols, cols)] = low

    fshot = assign_ref[s]
    ashot = assign_ref[groups + s]
    cells = recv_ref[pl.ds(ashot, 1), :]
    line, column = split_div(cells, cols)
    depth_id, row_id = split_div(line, rows_all)
    depth_id = depth_id - d * planes
    row_id = row_id - l * rows
    inside = (depth_id >= 0) & (depth_id < planes) & (row_id >= 0) & (row_id < rows)
    where_row = jnp.where(inside, depth_id * rows + row_id, -1)
    row_hot = jnp.where(
        lax.broadcasted_iota(jnp.int32, (planes * rows, n_rec), 0) == where_row, 1.0, 0.0
    ).astype(BF)
    col_hit = lax.broadcasted_iota(jnp.int32, (cols, n_rec), 0) == column
    traces = resid_ref[ashot]
    contract = (((1,), (1,)), ((), ()))
    for k in range(steps):
        part = jnp.where(col_hit, traces[k : k + 1, :], 0.0)
        amount = None
        for _ in range(3):
            piece = part.astype(BF)
            part = part - piece.astype(F32)
            term = lax.dot_general(row_hot, piece, contract, preferred_element_type=F32)
            amount = term if amount is None else amount + term
        inj[k] = amount.reshape(planes, rows, cols)

    sline, scol = split_div(source_ref[fshot], cols)
    sdepth, srow = split_div(sline, rows_all)
    sdepth = sdepth - d * planes
    srow = srow - l * rows
    sinside = (srow >= 0) & (srow < rows)
    sdepth = jnp.where(sinside, sdepth, -1)
    cell_ids = lax.broadcasted_iota(jnp.int32, (rows, cols), 0) * cols + lax.broadcasted_iota(
        jnp.int32, (rows, cols), 1
    )
    scell = srow * cols + scol

    def x_part(block):
        count = block.shape[0]
        block = block.reshape(count * rows, cols)
        high = block.astype(BF)
        low = (block - high.astype(F32)).astype(BF)
        lhs = jnp.concatenate([high, low, high], axis=1)
        return jnp.dot(lhs, wmat[...], preferred_element_type=F32)

    def imaging(k):
        def body(p, carry):
            older = states_v[k, p].astype(F32)
            mid = states_v[k + 1, p].astype(F32)
            newer = states_v[k + 2, p].astype(F32)
            term = ext[k % 2, ADJ, p + 4, core_r] * (newer - 2.0 * mid + older)
            img[p] = term if k == 0 else img[p] + term
            return carry

        lax.fori_loop(0, planes, body, 0)

    def diffs(pick, want_second=True):
        first = None
        second = None

        def add(total, tap, value):
            return tap * value if total is None else total + tap * value

        for reach in range(1, 5):
            f_tap, s_tap = FIRST_TAPS[reach - 1], SECOND_TAPS[reach - 1]
            ahead, behind = pick(reach), pick(-reach)
            if ahead is not None and behind is not None:
                first = add(first, f_tap, ahead - behind)
                if want_second:
                    second = add(second, s_tap, ahead + behind)
            elif ahead is not None or behind is not None:
                only = behind if ahead is None else ahead
                first = add(first, -f_tap if ahead is None else f_tap, only)
                second = add(second, s_tap, only)
        return first, second

    def coefficients(p0):
        xs = x_part(bext[pl.ds(p0 + 4, 4), core_r])
        for i in range(4):
            p = p0 + i
            m = model_v[p]
            sz, _ = diffs(lambda o: bext[p + 4 + o, core_r], False)
            sy, _ = diffs(lambda o: bext[p + 4, pl.ds(8 + o, rows)], False)
            coef[0, p] = m * bext[p + 4, core_r]
            coef[1, p] = m * sz
            coef[2, p] = m * sy
            coef[3, p] = m * xs[i * rows : (i + 1) * rows, cols:]

    def target(k, f, p):
        if k == steps - 1:
            return outs[f].at[0, 1, p]
        return ext.at[(k + 1) % 2, f, p + 4, core_r]

    def x_all(k, f):
        xder[f] = x_part(ext[k % 2, f, core_p, core_r])

    def advance(k, f, p0, side=None):
        now, then = k % 2, (k + 1) % 2
        for i in range(4):
            p = p0 + i

            def z_pick(o):
                if side == 0 and i + o < 0 or side == 1 and i + o > 3:
                    return None
                return ext[now, f, p + 4 + o, core_r]

            fz, gz = diffs(z_pick)
            fy, gy = diffs(lambda o: ext[now, f, p + 4, pl.ds(8 + o, rows)])
            xrow = pl.ds(p * rows, rows)
            value = (
                2.0 * ext[now, f, p + 4, core_r]
                - ext[then, f, p + 4, core_r]
                + coef[0, p] * (gz + gy + xder[f, xrow, pl.ds(0, cols)])
                + coef[1, p] * fz
                + coef[2, p] * fy
                + coef[3, p] * xder[f, xrow, pl.ds(cols, cols)]
            )
            if f == ADJ:
                value = value + inj[k, p]
            else:
                here = jnp.where(sdepth == p, scell, -1)
                value = value + jnp.where(cell_ids == here, wave_ref[fshot, k], 0.0)
            target(k, f, p)[...] = value

    def add_halo(k, f, side):
        now = k % 2
        p0 = chunks[side][0]
        for i in range(4):
            p = p0 + i

            def z_pick(o):
                if side == 0 and i + o < 0 or side == 1 and i + o > 3:
                    return ext[now, f, p + 4 + o, core_r]
                return None

            fz, gz = diffs(z_pick)
            place = target(k, f, p)
            place[...] = place[...] + (coef[0, p] * gz + coef[1, p] * fz)

    loads["states"].wait()
    loads[("cur", ADJ)].wait()
    imaging(0)
    loads["model"].wait()
    loads["buoy"].wait()
    for way in (0, 1):
        wait_recv(bcopy("lat", way), "lat", way)

    def coef_body(c, carry):
        coefficients(c * 4)
        return carry

    lax.fori_loop(1, planes // 4 - 1, coef_body, 0)
    for way in (0, 1):
        wait_recv(bcopy("depth", way), "depth", way)
    coefficients(0)
    coefficients(planes - 4)
    loads[("prev", ADJ)].wait()
    loads[("cur", FWD)].wait()
    loads[("prev", FWD)].wait()

    def share_copy(o):
        dest = lax.rem(s + o, groups)
        return pltpu.make_async_remote_copy(
            src_ref=img.at[pl.ds(dest * q, q)], dst_ref=share.at[o - 1],
            send_sem=ssend.at[o - 1], recv_sem=srecv.at[o - 1],
            device_id={"shot": dest}, device_id_type=MESH,
        )

    for k in range(steps):
        last = k == steps - 1
        if k > 0:
            imaging(k)
        if last:
            for o in range(1, groups):
                share_copy(o).start()
        for f in (ADJ, FWD):
            x_all(k, f)
            if k >= 2:
                for way in (0, 1):
                    wait_send(zcopy(k - 1, f, way), "depth", way)
                    for c in range(len(chunks)):
                        wait_send(ycopy(k - 1, f, c, way), "lat", way)
            for c in (0, 1):
                for way in (0, 1):
                    wait_recv(ycopy(k, f, c, way), "lat", way)
                advance(k, f, chunks[c][0], c)
        for f in (ADJ, FWD):
            for c in (0, 1):
                wait_recv(zcopy(k, f, 1 - c), "depth", 1 - c)
                add_halo(k, f, c)
                if not last:
                    start(zcopy(k + 1, f, c), "depth", c)
                    for way in (0, 1):
                        start(ycopy(k + 1, f, c, way), "lat", way)
        for f in (ADJ, FWD):
            if len(chunks) > 2:
                for way in (0, 1):
                    wait_recv(ycopy(k, f, 2, way), "lat", way)

                def inner(c, carry):
                    advance(k, f, 4 + c * 4)
                    return carry

                lax.fori_loop(0, (planes - 8) // 4, inner, 0)
                if not last:
                    for way in (0, 1):
                        start(ycopy(k + 1, f, 2, way), "lat", way)
            if last:
                outs[f][0, 0] = ext[k % 2, f, core_p, core_r]

    loads["mom"].wait()
    for o in range(1, groups):
        share_copy(o).wait_recv()
    factor = 1.0 / (groups * steps)
    for p in range(q):
        gradient = img[s * q + p]
        for o in range(1, groups):
            gradient = gradient + share[o - 1, p]
        moment = MOMENT_KEEP * mom_v[p] + factor * gradient
        momout_ref[p] = moment
        modout_ref[p] = model_v[s * q + p] - STEP_RATE * moment
    for o in range(1, groups):
        share_copy(o).wait_send()
    for way in (0, 1):
        wait_send(bcopy("depth", way), "depth", way)
        wait_send(bcopy("lat", way), "lat", way)
    for e in sorted({0, steps - 1}):
        for f in (ADJ, FWD):
            for way in (0, 1):
                wait_send(zcopy(e, f, way), "depth", way)
                for c in range(len(chunks)):
                    wait_send(ycopy(e, f, c, way), "lat", way)


def to_memory(*refs):
    count = (len(refs) - 1) // 2
    sems = refs[-1]
    copies = [
        pltpu.make_async_copy(refs[i], refs[count + i], sems.at[i]) for i in range(count)
    ]
    for copy in copies:
        copy.start()
    for copy in copies:
        copy.wait()


def local(
    model_field, buoyancy, forward_pair, adjoint_pair, stored_states, momentum,
    wavelet, residuals, source_cells, receiver_cells, assignment,
):
    groups = lax.axis_size("shot")
    n_depth = lax.axis_size("depth")
    n_lat = lax.axis_size("lat")
    planes, rows, cols = model_field.shape
    steps = stored_states.shape[1] - 2
    n_rec = receiver_cells.shape[1]
    q = planes // groups
    dims = (groups, n_depth, n_lat, planes, rows, cols, steps, n_rec)
    smem = pl.BlockSpec(memory_space=pltpu.SMEM)
    vmem = pl.BlockSpec(memory_space=pltpu.VMEM)
    hbm = pl.BlockSpec(memory_space=pltpu.HBM)
    dma = pltpu.SemaphoreType.DMA
    block = (planes, rows, cols)
    others = max(groups - 1, 1)
    out_dims = (forward_pair.shape, adjoint_pair.shape, momentum.shape, momentum.shape)
    out = pl.pallas_call(
        functools.partial(kernel, dims),
        out_shape=tuple(pltpu.VMEM(shape, F32) for shape in out_dims),
        in_specs=[smem, smem, smem, vmem, vmem] + [hbm] * 6,
        out_specs=(vmem,) * 4,
        scratch_shapes=[
            pltpu.VMEM((2, 2, planes + 8, rows + 16, cols), F32),
            pltpu.VMEM((planes + 8, rows + 16, cols), F32),
            pltpu.VMEM(block, F32),
            pltpu.VMEM((steps + 2,) + block, BF),
            pltpu.VMEM((q, rows, cols), F32),
            pltpu.VMEM((4,) + block, F32),
            pltpu.VMEM((steps,) + block, F32),
            pltpu.VMEM((2, planes * rows, 2 * cols), F32),
            pltpu.VMEM(block, F32),
            pltpu.VMEM((others, q, rows, cols), F32),
            pltpu.VMEM((3 * cols, 2 * cols), BF),
            dma((steps, 2, 2)), dma((steps, 2, 2)),
            dma((steps, 2, 3, 2)), dma((steps, 2, 3, 2)),
            dma((2, 2)), dma((2, 2)),
            dma((others,)), dma((others,)),
            dma((8,)),
        ],
        compiler_params=pltpu.CompilerParams(
            collective_id=0, has_side_effects=True, vmem_limit_bytes=VMEM_WINDOW
        ),
    )(
        assignment, source_cells, wavelet, receiver_cells, residuals,
        model_field, buoyancy, forward_pair, adjoint_pair, stored_states, momentum,
    )
    return pl.pallas_call(
        to_memory,
        out_shape=tuple(jax.ShapeDtypeStruct(shape, F32) for shape in out_dims),
        in_specs=[vmem] * 4,
        out_specs=(hbm,) * 4,
        scratch_shapes=[dma((4,))],
        compiler_params=pltpu.CompilerParams(vmem_limit_bytes=VMEM_OUT),
    )(*out)


def solution(mesh):
    in_specs = (
        P(("inv", "depth"), "lat", None),
        P(("inv", "depth"), "lat", None),
        P(("inv", "shot"), None, "depth", "lat", None),
        P(("inv", "shot"), None, "depth", "lat", None),
        P(("inv", "shot"), None, "depth", "lat", None),
        P(("inv", "depth", "shot"), "lat", None),
        P("inv", None),
        P("inv", None, None),
        P("inv"),
        P("inv", None),
        P("inv"),
    )
    out_specs = (
        P(("inv", "shot"), None, "depth", "lat", None),
        P(("inv", "shot"), None, "depth", "lat", None),
        P(("inv", "depth", "shot"), "lat", None),
        P(("inv", "depth", "shot"), "lat", None),
    )
    return jax.shard_map(local, mesh=mesh, in_specs=in_specs, out_specs=out_specs, check_vma=False)
```

```python
import functools
import jax
import jax.numpy as jnp
from jax import lax
from jax.experimental import pallas as pl
from jax.experimental.pallas import tpu as pltpu
from jax.sharding import PartitionSpec as P

SECOND_TAPS = (8.0 / 5.0, -1.0 / 5.0, 8.0 / 315.0, -1.0 / 560.0)
CENTER_TAP = -205.0 / 72.0
FIRST_TAPS = (4.0 / 5.0, -1.0 / 5.0, 4.0 / 105.0, -1.0 / 280.0)
MOMENT_KEEP = 0.9
STEP_RATE = 0.02
MESH = pl.DeviceIdType.MESH
BF = jnp.bfloat16
F32 = jnp.float32
FWD, ADJ = 0, 1
VMEM_WINDOW = 61 * 1024 * 1024
VMEM_OUT = 24 * 1024 * 1024


def split_div(value, size):
    if size & (size - 1) == 0:
        bits = size.bit_length() - 1
        return lax.shift_right_logical(value, bits), value & (size - 1)
    whole = lax.div(value, size)
    return whole, value - whole * size


def kernel(
    dims,
    assign_ref, source_ref, wave_ref, recv_ref, resid_ref,
    model_ref, buoy_ref, fpair_ref, apair_ref, states_ref, mom_ref,
    fout_ref, aout_ref, momout_ref, modout_ref,
    ext, bext, model_v, states_v, mom_v, coef, inj, xder, img, share, wmat,
    zsend, zrecv, ysend, yrecv, bsend, brecv, ssend, srecv, load,
):
    groups, n_depth, n_lat, planes, rows, cols, steps, n_rec = dims
    rows_all = rows * n_lat
    q = planes // groups
    d = lax.axis_index("depth")
    l = lax.axis_index("lat")
    s = lax.axis_index("shot")
    pairs = (fpair_ref, apair_ref)
    outs = (fout_ref, aout_ref)
    core_p = pl.ds(4, planes)
    core_r = pl.ds(8, rows)
    has = {
        ("depth", 0): d > 0,
        ("depth", 1): d < n_depth - 1,
        ("lat", 0): l > 0,
        ("lat", 1): l < n_lat - 1,
    }
    rank = {"depth": d, "lat": l}

    loads = {}

    def begin(name, src, dst):
        loads[name] = pltpu.make_async_copy(src, dst, load.at[len(loads)])
        loads[name].start()

    begin("buoy", buoy_ref, bext.at[core_p, core_r])
    begin("model", model_ref, model_v)
    for f in (ADJ, FWD):
        begin(("cur", f), pairs[f].at[0, 1], ext.at[0, f, core_p, core_r])
        begin(("prev", f), pairs[f].at[0, 0], ext.at[1, f, core_p, core_r])
    begin("states", states_ref.at[0], states_v)
    begin("mom", mom_ref, mom_v)

    barrier = pltpu.get_barrier_semaphore()
    total = groups - 1
    for (axis, way), there in has.items():
        total = total + there.astype(jnp.int32)

        @pl.when(there)
        def _(axis=axis, way=way):
            pl.semaphore_signal(
                barrier, inc=1, device_id={axis: rank[axis] + 2 * way - 1}, device_id_type=MESH
            )

    for o in range(1, groups):
        pl.semaphore_signal(
            barrier, inc=1, device_id={"shot": lax.rem(s + o, groups)}, device_id_type=MESH
        )
    pl.semaphore_wait(barrier, total)

    def remote(src, dst, send, recv, axis, way):
        return pltpu.make_async_remote_copy(
            src_ref=src, dst_ref=dst, send_sem=send, recv_sem=recv,
            device_id={axis: rank[axis] + 2 * way - 1}, device_id_type=MESH,
        )

    chunks = ((0, 4), (planes - 4, 4)) + (((4, planes - 8),) if planes > 8 else ())

    def zcopy(e, f, way):
        slot = e % 2
        first = planes - 4 if way else 0
        if e == 0:
            src = pairs[f].at[0, 1, pl.ds(first, 4)]
        else:
            src = ext.at[slot, f, pl.ds(4 + first, 4), core_r]
        dst = ext.at[slot, f, pl.ds(0 if way else planes + 4, 4), core_r]
        return remote(src, dst, zsend.at[e, f, way], zrecv.at[e, f, way], "depth", way)

    def ycopy(e, f, c, way):
        slot = e % 2
        first, count = chunks[c]
        row = rows - 8 if way else 0
        if e == 0:
            src = pairs[f].at[0, 1, pl.ds(first, count), pl.ds(row, 8)]
        else:
            src = ext.at[slot, f, pl.ds(4 + first, count), pl.ds(8 + row, 8)]
        dst = ext.at[slot, f, pl.ds(4 + first, count), pl.ds(0 if way else rows + 8, 8)]
        return remote(src, dst, ysend.at[e, f, c, way], yrecv.at[e, f, c, way], "lat", way)

    def bcopy(axis, way):
        a = 0 if axis == "depth" else 1
        if a == 0:
            src = buoy_ref.at[pl.ds(planes - 4 if way else 0, 4)]
            dst = bext.at[pl.ds(0 if way else planes + 4, 4), core_r]
        else:
            src = buoy_ref.at[:, pl.ds(rows - 8 if way else 0, 8)]
            dst = bext.at[core_p, pl.ds(0 if way else rows + 8, 8)]
        return remote(src, dst, bsend.at[a, way], brecv.at[a, way], axis, way)

    def start(copy, axis, way):
        @pl.when(has[(axis, way)])
        def _():
            copy.start()

    def wait_send(copy, axis, way):
        @pl.when(has[(axis, way)])
        def _():
            copy.wait_send()

    def wait_recv(copy, axis, way):
        @pl.when(has[(axis, 1 - way)])
        def _():
            copy.wait_recv()

    for way in (0, 1):
        start(bcopy("depth", way), "depth", way)
        start(bcopy("lat", way), "lat", way)
    for f in (ADJ, FWD):
        for way in (0, 1):
            start(zcopy(0, f, way), "depth", way)
            for c in range(len(chunks)):
                start(ycopy(0, f, c, way), "lat", way)

    for way, lo in ((0, 0), (1, planes + 4)):

        @pl.when(jnp.logical_not(has[("depth", way)]))
        def _(lo=lo):
            for f in range(2):
                for slot in range(2):
                    ext[slot, f, pl.ds(lo, 4), core_r] = jnp.zeros((4, rows, cols), F32)
            bext[pl.ds(lo, 4), core_r] = jnp.zeros((4, rows, cols), F32)

    for way, lo in ((0, 0), (1, rows + 8)):

        @pl.when(jnp.logical_not(has[("lat", way)]))
        def _(lo=lo):
            for f in range(2):
                for slot in range(2):
                    ext[slot, f, core_p, pl.ds(lo, 8)] = jnp.zeros((planes, 8, cols), F32)
            bext[core_p, pl.ds(lo, 8)] = jnp.zeros((planes, 8, cols), F32)

    delta = lax.broadcasted_iota(jnp.int32, (cols, cols), 0) - lax.broadcasted_iota(
        jnp.int32, (cols, cols), 1
    )
    second = jnp.where(delta == 0, 3.0 * CENTER_TAP, 0.0).astype(F32)
    first = jnp.zeros((cols, cols), F32)
    for reach in range(1, 5):
        second = jnp.where(jnp.abs(delta) == reach, SECOND_TAPS[reach - 1], second)
        first = jnp.where(delta == reach, FIRST_TAPS[reach - 1], first)
        first = jnp.where(delta == -reach, -FIRST_TAPS[reach - 1], first)
    for a, mat in ((0, second), (1, first)):
        high = mat.astype(BF)
        low = (mat - high.astype(F32)).astype(BF)
        wmat[pl.ds(0, cols), pl.ds(a * cols, cols)] = high
        wmat[pl.ds(cols, cols), pl.ds(a * cols, cols)] = high
        wmat[pl.ds(2 * cols, cols), pl.ds(a * cols, cols)] = low

    fshot = assign_ref[s]
    ashot = assign_ref[groups + s]
    cells = recv_ref[pl.ds(ashot, 1), :]
    line, column = split_div(cells, cols)
    depth_id, row_id = split_div(line, rows_all)
    depth_id = depth_id - d * planes
    row_id = row_id - l * rows
    inside = (depth_id >= 0) & (depth_id < planes) & (row_id >= 0) & (row_id < rows)
    where_row = jnp.where(inside, depth_id * rows + row_id, -1)
    row_hot = jnp.where(
        lax.broadcasted_iota(jnp.int32, (planes * rows, n_rec), 0) == where_row, 1.0, 0.0
    ).astype(BF)
    col_hit = lax.broadcasted_iota(jnp.int32, (cols, n_rec), 0) == column
    traces = resid_ref[ashot]
    contract = (((1,), (1,)), ((), ()))
    for k in range(steps):
        part = jnp.where(col_hit, traces[k : k + 1, :], 0.0)
        amount = None
        for _ in range(3):
            piece = part.astype(BF)
            part = part - piece.astype(F32)
            term = lax.dot_general(row_hot, piece, contract, preferred_element_type=F32)
            amount = term if amount is None else amount + term
        inj[k] = amount.reshape(planes, rows, cols)

    sline, scol = split_div(source_ref[fshot], cols)
    sdepth, srow = split_div(sline, rows_all)
    sdepth = sdepth - d * planes
    srow = srow - l * rows
    sinside = (srow >= 0) & (srow < rows)
    sdepth = jnp.where(sinside, sdepth, -1)
    cell_ids = lax.broadcasted_iota(jnp.int32, (rows, cols), 0) * cols + lax.broadcasted_iota(
        jnp.int32, (rows, cols), 1
    )
    scell = srow * cols + scol

    def x_part(block):
        count = block.shape[0]
        block = block.reshape(count * rows, cols)
        high = block.astype(BF)
        low = (block - high.astype(F32)).astype(BF)
        lhs = jnp.concatenate([high, low, high], axis=1)
        return jnp.dot(lhs, wmat[...], preferred_element_type=F32)

    def imaging(k):
        def body(p, carry):
            older = states_v[k, p].astype(F32)
            mid = states_v[k + 1, p].astype(F32)
            newer = states_v[k + 2, p].astype(F32)
            term = ext[k % 2, ADJ, p + 4, core_r] * (newer - 2.0 * mid + older)
            img[p] = term if k == 0 else img[p] + term
            return carry

        lax.fori_loop(0, planes, body, 0)

    def diffs(pick, want_second=True):
        first = None
        second = None

        def add(total, tap, value):
            return tap * value if total is None else total + tap * value

        for reach in range(1, 5):
            f_tap, s_tap = FIRST_TAPS[reach - 1], SECOND_TAPS[reach - 1]
            ahead, behind = pick(reach), pick(-reach)
            if ahead is not None and behind is not None:
                first = add(first, f_tap, ahead - behind)
                if want_second:
                    second = add(second, s_tap, ahead + behind)
            elif ahead is not None or behind is not None:
                only = behind if ahead is None else ahead
                first = add(first, -f_tap if ahead is None else f_tap, only)
                second = add(second, s_tap, only)
        return first, second

    def coefficients(p0):
        xs = x_part(bext[pl.ds(p0 + 4, 4), core_r])
        for i in range(4):
            p = p0 + i
            m = model_v[p]
            sz, _ = diffs(lambda o: bext[p + 4 + o, core_r], False)
            sy, _ = diffs(lambda o: bext[p + 4, pl.ds(8 + o, rows)], False)
            coef[0, p] = m * bext[p + 4, core_r]
            coef[1, p] = m * sz
            coef[2, p] = m * sy
            coef[3, p] = m * xs[i * rows : (i + 1) * rows, cols:]

    def target(k, f, p):
        if k == steps - 1:
            return outs[f].at[0, 1, p]
        return ext.at[(k + 1) % 2, f, p + 4, core_r]

    def x_all(k, f):
        xder[f] = x_part(ext[k % 2, f, core_p, core_r])

    def advance(k, f, p0, side=None):
        now, then = k % 2, (k + 1) % 2
        for i in range(4):
            p = p0 + i

            def z_pick(o):
                if side == 0 and i + o < 0 or side == 1 and i + o > 3:
                    return None
                return ext[now, f, p + 4 + o, core_r]

            fz, gz = diffs(z_pick)
            fy, gy = diffs(lambda o: ext[now, f, p + 4, pl.ds(8 + o, rows)])
            xrow = pl.ds(p * rows, rows)
            value = (
                2.0 * ext[now, f, p + 4, core_r]
                - ext[then, f, p + 4, core_r]
                + coef[0, p] * (gz + gy + xder[f, xrow, pl.ds(0, cols)])
                + coef[1, p] * fz
                + coef[2, p] * fy
                + coef[3, p] * xder[f, xrow, pl.ds(cols, cols)]
            )
            if f == ADJ:
                value = value + inj[k, p]
            else:
                here = jnp.where(sdepth == p, scell, -1)
                value = value + jnp.where(cell_ids == here, wave_ref[fshot, k], 0.0)
            target(k, f, p)[...] = value

    def add_halo(k, f, side):
        now = k % 2
        p0 = chunks[side][0]
        for i in range(4):
            p = p0 + i

            def z_pick(o):
                if side == 0 and i + o < 0 or side == 1 and i + o > 3:
                    return ext[now, f, p + 4 + o, core_r]
                return None

            fz, gz = diffs(z_pick)
            place = target(k, f, p)
            place[...] = place[...] + (coef[0, p] * gz + coef[1, p] * fz)

    loads["states"].wait()
    loads[("cur", ADJ)].wait()
    imaging(0)
    loads["model"].wait()
    loads["buoy"].wait()
    for way in (0, 1):
        wait_recv(bcopy("lat", way), "lat", way)

    def coef_body(c, carry):
        coefficients(c * 4)
        return carry

    lax.fori_loop(1, planes // 4 - 1, coef_body, 0)
    for way in (0, 1):
        wait_recv(bcopy("depth", way), "depth", way)
    coefficients(0)
    coefficients(planes - 4)
    loads[("prev", ADJ)].wait()
    loads[("cur", FWD)].wait()
    loads[("prev", FWD)].wait()

    def share_copy(o):
        dest = lax.rem(s + o, groups)
        return pltpu.make_async_remote_copy(
            src_ref=img.at[pl.ds(dest * q, q)], dst_ref=share.at[o - 1],
            send_sem=ssend.at[o - 1], recv_sem=srecv.at[o - 1],
            device_id={"shot": dest}, device_id_type=MESH,
        )

    for k in range(steps):
        last = k == steps - 1
        if 0 < k and (steps < 2 or not last):
            imaging(k)
        if last and steps < 2:
            for o in range(1, groups):
                share_copy(o).start()
        for f in (ADJ, FWD):
            x_all(k, f)
            if k >= 2:
                for way in (0, 1):
                    wait_send(zcopy(k - 1, f, way), "depth", way)
                    for c in range(len(chunks)):
                        wait_send(ycopy(k - 1, f, c, way), "lat", way)
            for c in (0, 1):
                for way in (0, 1):
                    wait_recv(ycopy(k, f, c, way), "lat", way)
                advance(k, f, chunks[c][0], c)
        for f in (ADJ, FWD):
            for c in (0, 1):
                wait_recv(zcopy(k, f, 1 - c), "depth", 1 - c)
                add_halo(k, f, c)
                if not last:
                    start(zcopy(k + 1, f, c), "depth", c)
                    for way in (0, 1):
                        start(ycopy(k + 1, f, c, way), "lat", way)
            if len(chunks) > 2:
                for way in (0, 1):
                    wait_recv(ycopy(k, f, 2, way), "lat", way)

                def inner(c, carry):
                    advance(k, f, 4 + c * 4)
                    return carry

                lax.fori_loop(0, (planes - 8) // 4, inner, 0)
                if not last:
                    for way in (0, 1):
                        start(ycopy(k + 1, f, 2, way), "lat", way)
            if f == ADJ and k == steps - 2:
                imaging(steps - 1)
                for o in range(1, groups):
                    share_copy(o).start()
            if last:
                outs[f][0, 0] = ext[k % 2, f, core_p, core_r]

    loads["mom"].wait()
    for o in range(1, groups):
        share_copy(o).wait_recv()
    factor = 1.0 / (groups * steps)
    for p in range(q):
        gradient = img[s * q + p]
        for o in range(1, groups):
            gradient = gradient + share[o - 1, p]
        moment = MOMENT_KEEP * mom_v[p] + factor * gradient
        momout_ref[p] = moment
        modout_ref[p] = model_v[s * q + p] - STEP_RATE * moment
    for o in range(1, groups):
        share_copy(o).wait_send()
    for way in (0, 1):
        wait_send(bcopy("depth", way), "depth", way)
        wait_send(bcopy("lat", way), "lat", way)
    for e in sorted({0, steps - 1}):
        for f in (ADJ, FWD):
            for way in (0, 1):
                wait_send(zcopy(e, f, way), "depth", way)
                for c in range(len(chunks)):
                    wait_send(ycopy(e, f, c, way), "lat", way)


def to_memory(*refs):
    count = (len(refs) - 1) // 2
    sems = refs[-1]
    copies = [
        pltpu.make_async_copy(refs[i], refs[count + i], sems.at[i]) for i in range(count)
    ]
    for copy in copies:
        copy.start()
    for copy in copies:
        copy.wait()


def local(
    model_field, buoyancy, forward_pair, adjoint_pair, stored_states, momentum,
    wavelet, residuals, source_cells, receiver_cells, assignment,
):
    groups = lax.axis_size("shot")
    n_depth = lax.axis_size("depth")
    n_lat = lax.axis_size("lat")
    planes, rows, cols = model_field.shape
    steps = stored_states.shape[1] - 2
    n_rec = receiver_cells.shape[1]
    q = planes // groups
    dims = (groups, n_depth, n_lat, planes, rows, cols, steps, n_rec)
    smem = pl.BlockSpec(memory_space=pltpu.SMEM)
    vmem = pl.BlockSpec(memory_space=pltpu.VMEM)
    hbm = pl.BlockSpec(memory_space=pltpu.HBM)
    dma = pltpu.SemaphoreType.DMA
    block = (planes, rows, cols)
    others = max(groups - 1, 1)
    out_dims = (forward_pair.shape, adjoint_pair.shape, momentum.shape, momentum.shape)
    out = pl.pallas_call(
        functools.partial(kernel, dims),
        out_shape=tuple(pltpu.VMEM(shape, F32) for shape in out_dims),
        in_specs=[smem, smem, smem, vmem, vmem] + [hbm] * 6,
        out_specs=(vmem,) * 4,
        scratch_shapes=[
            pltpu.VMEM((2, 2, planes + 8, rows + 16, cols), F32),
            pltpu.VMEM((planes + 8, rows + 16, cols), F32),
            pltpu.VMEM(block, F32),
            pltpu.VMEM((steps + 2,) + block, BF),
            pltpu.VMEM((q, rows, cols), F32),
            pltpu.VMEM((4,) + block, F32),
            pltpu.VMEM((steps,) + block, F32),
            pltpu.VMEM((2, planes * rows, 2 * cols), F32),
            pltpu.VMEM(block, F32),
            pltpu.VMEM((others, q, rows, cols), F32),
            pltpu.VMEM((3 * cols, 2 * cols), BF),
            dma((steps, 2, 2)), dma((steps, 2, 2)),
            dma((steps, 2, 3, 2)), dma((steps, 2, 3, 2)),
            dma((2, 2)), dma((2, 2)),
            dma((others,)), dma((others,)),
            dma((8,)),
        ],
        compiler_params=pltpu.CompilerParams(
            collective_id=0, has_side_effects=True, vmem_limit_bytes=VMEM_WINDOW
        ),
    )(
        assignment, source_cells, wavelet, receiver_cells, residuals,
        model_field, buoyancy, forward_pair, adjoint_pair, stored_states, momentum,
    )
    return pl.pallas_call(
        to_memory,
        out_shape=tuple(jax.ShapeDtypeStruct(shape, F32) for shape in out_dims),
        in_specs=[vmem] * 4,
        out_specs=(hbm,) * 4,
        scratch_shapes=[dma((4,))],
        compiler_params=pltpu.CompilerParams(vmem_limit_bytes=VMEM_OUT),
    )(*out)


def solution(mesh):
    in_specs = (
        P(("inv", "depth"), "lat", None),
        P(("inv", "depth"), "lat", None),
        P(("inv", "shot"), None, "depth", "lat", None),
        P(("inv", "shot"), None, "depth", "lat", None),
        P(("inv", "shot"), None, "depth", "lat", None),
        P(("inv", "depth", "shot"), "lat", None),
        P("inv", None),
        P("inv", None, None),
        P("inv"),
        P("inv", None),
        P("inv"),
    )
    out_specs = (
        P(("inv", "shot"), None, "depth", "lat", None),
        P(("inv", "shot"), None, "depth", "lat", None),
        P(("inv", "depth", "shot"), "lat", None),
        P(("inv", "depth", "shot"), "lat", None),
    )
    return jax.shard_map(local, mesh=mesh, in_specs=in_specs, out_specs=out_specs, check_vma=False)
```
